32 devices in a mesh: leaf: 8 (over z, core), rep: 4 (over y, x).
Axes of the slice: x: 2, y: 2, z: 4, core: 2. Of those that a mesh axis runs over, the one named last changes fastest.
Arguments:
- curve_coordinates: float32 [2, 65536], P(None, 'leaf'), may hold values from -1.25 to 1.25, as said below
- weighted_density: float32 [65536], P('leaf'), may hold values from 0.02 to 0.2
- random_test_matrix: float32 [128, 65536], P('rep', 'leaf'), may hold values from -6 to 6
- sketch_matrix: float32 [128, 65536], P('rep', 'leaf'), may hold values from -12 to 12
Outputs:
- leaf_basis: float32 [128, 65536], P('rep', 'leaf')
- top_basis: float32 [8, 128, 256], P('leaf', 'rep')
The draws below stay inside these ranges and needn't reach their ends.
Inputs may be any that keep to these rules, and one draw needn't show every extreme that they name: `curve_coordinates`: the points are in order along one closed smooth curve, one point in each of 65536 equal parameter cells.
All inputs are finite; a program needn't handle non-finite values.
Results may differ from the reference program's by a relative error of at most 0.00035.
Values sent between devices are 32-bit elements; how exact they have to be, the bound alone decides.
A program may use at most 64 MiB of HBM per device.

```python
import math
import jax
import jax.numpy as jnp
from jax import lax

NODES_PER_CELL = 512
S = 128
LEAF_LEVELS = 4
CROSS = 3
CURVE_NODE_NUM = 65536


def draw_curve_coordinates(key, part):
    position = jnp.arange(CURVE_NODE_NUM, dtype=jnp.float32)
    jitter = jax.random.uniform(key, (CURVE_NODE_NUM,), jnp.float32, -0.3, 0.3)
    angle_rad = 2.0 * math.pi * (position + 0.5 + jitter) / CURVE_NODE_NUM
    radius = 1.0 + 0.2 * jnp.cos(5.0 * angle_rad)
    return jnp.stack([radius * jnp.cos(angle_rad), radius * jnp.sin(angle_rad)])


def steps_of(own_key, shape, shards, smallest, top_value):
    loudness = 1.0
    for axis_at, parts in shards:
        steps = jax.random.uniform(jax.random.fold_in(jax.random.fold_in(own_key, 6), axis_at), (parts,), jnp.float32, smallest / len(shards), top_value / len(shards))
        loudness = loudness * jnp.repeat(jnp.exp(steps), shape[axis_at] // parts).reshape((-1,) + (1,) * (len(shape) - 1 - axis_at))
    return loudness


def bell_draw(rng, dims, deviation, reach, split=(), held_as=jnp.bfloat16):
    result = deviation * jax.random.normal(rng, dims, jnp.float32)
    if split:
        result = result * steps_of(rng, dims, split, -0.22, 0.18)
    return jnp.clip(result, -reach, reach).astype(held_as)


def setup_inputs(seed: int = 0) -> dict:
    streams_of = jax.random.split(jax.random.key(seed), 5)
    curve_coordinates = draw_curve_coordinates(jax.random.fold_in(streams_of[4], 71), 0)
    weighted_density = jnp.clip(jnp.exp(math.log(0.2) - 2.3025851 * jax.random.uniform(streams_of[1], (CURVE_NODE_NUM,), jnp.float32) ** steps_of(streams_of[1], (CURVE_NODE_NUM,), ((0, 8),), -0.2, 0.2)), 0.02, 0.2)
    random_test_matrix = bell_draw(streams_of[2], (S, CURVE_NODE_NUM), 1.0, 6.0, ((0, 4), (1, 8)), jnp.float32)
    sketch_matrix = bell_draw(streams_of[3], (S, CURVE_NODE_NUM), 2.0, 12.0, ((0, 4), (1, 8)), jnp.float32)
    return {"curve_coordinates": curve_coordinates, "weighted_density": weighted_density, "random_test_matrix": random_test_matrix, "sketch_matrix": sketch_matrix}


grouping = 4

def distances(targets, sources):
    delta_x = targets[0][:, None] - sources[0][None, :]
    delta_y = targets[1][:, None] - sources[1][None, :]
    return delta_x * delta_x + delta_y * delta_y

def near_field(window, blocks):
    span = window.shape[2]
    height = window.shape[1]
    row_ids = lax.broadcasted_iota(jnp.int32, (span, 3 * span), 0)
    col_ids = lax.broadcasted_iota(jnp.int32, (span, 3 * span), 1)
    same = row_ids + span == col_ids
    results = []
    for offset in range(blocks):
        sources = window[offset:offset + 3].transpose(1, 0, 2).reshape(height, 3 * span)
        targets = window[offset + 1, :2]
        squared = distances(targets, sources[:2])
        guarded = jnp.where(same, 1.0, squared)
        potential = jnp.log(guarded) * (-0.25 / math.pi)
        self_term = (1.0 - jnp.log(0.5 * sources[2])) * (0.5 / math.pi)
        matrix = jnp.where(same, self_term[None, :], potential) * sources[2][None, :]
        results.append(jnp.einsum('cj,ij->ci', sources[3:], matrix, precision=lax.Precision.HIGHEST))
    return jnp.stack(results)

def couple(skel_rows, skel_cols):

    def single(rows, cols):
        return jnp.log(distances(rows[:2], cols[:2])) * (-0.25 / math.pi) * cols[2][None, :]
    return jax.vmap(single)(skel_rows, skel_cols)

def assemble(sample_hat, probe_hat, skeleton):
    upper_y, lower_y = (sample_hat[0::2], sample_hat[1::2])
    upper_w, lower_w = (probe_hat[0::2], probe_hat[1::2])
    upper_s, lower_s = (skeleton[0::2], skeleton[1::2])
    cross_ab = couple(upper_s, lower_s)
    cross_ba = couple(lower_s, upper_s)
    top_rows = upper_y - jnp.einsum('nct,nst->ncs', lower_w, cross_ab, precision=lax.Precision.HIGHEST)
    bottom_rows = lower_y - jnp.einsum('nct,nst->ncs', upper_w, cross_ba, precision=lax.Precision.HIGHEST)
    off_diag = jnp.concatenate([top_rows, bottom_rows], 2)
    joined_y = jnp.concatenate([upper_y, lower_y], 2)
    joined_w = jnp.concatenate([upper_w, lower_w], 2)
    joined_s = jnp.concatenate([upper_s, lower_s], 2)[:, :, ::2]
    parent_s = jnp.concatenate([joined_s[:, :2], 2.0 * joined_s[:, 2:]], 1)
    return (off_diag, joined_y, joined_w, parent_s)

def project(basis_rows, stacked):
    return jnp.einsum('nsm,ncm->ncs', basis_rows, stacked, precision=lax.Precision.HIGHEST)

def orthonormal(off_diag):
    gram = jnp.einsum('nsm,ntm->nst', off_diag, off_diag, precision=lax.Precision.HIGHEST)
    factor = jnp.linalg.cholesky(gram)
    order = gram.shape[1]
    identity = jnp.eye(order, dtype=gram.dtype)
    inverse = jax.vmap(lambda low: jax.scipy.linalg.solve_triangular(low, identity, lower=True))(factor)
    return jnp.einsum('nst,ntm->nsm', inverse, off_diag, precision=lax.Precision.HIGHEST)

def reference(curve_coordinates, weighted_density, random_test_matrix, sketch_matrix):
    total = curve_coordinates.shape[1]
    number_finest_cells = total // NODES_PER_CELL
    step_width = NODES_PER_CELL // S
    finest_cell_coordinates = curve_coordinates.reshape(2, number_finest_cells, NODES_PER_CELL).transpose(1, 0, 2)
    finest_cell_weights = weighted_density.reshape(number_finest_cells, 1, NODES_PER_CELL)
    finest_cell_random_test = random_test_matrix.reshape(S, number_finest_cells, NODES_PER_CELL).transpose(1, 0, 2)
    leaf_y = sketch_matrix.reshape(S, number_finest_cells, NODES_PER_CELL).transpose(1, 0, 2)
    scratch_buffer = jnp.concatenate([finest_cell_coordinates, finest_cell_weights, finest_cell_random_test], 1)
    padded_rows = jnp.concatenate([scratch_buffer[-1:], scratch_buffer, scratch_buffer[:1]], 0)

    def block_near(block_index):
        window = lax.dynamic_slice_in_dim(padded_rows, block_index * grouping, grouping + 2, 0)
        return near_field(window, grouping)
    near = lax.map(block_near, jnp.arange(number_finest_cells // grouping, dtype=jnp.int32))
    near = near.reshape(number_finest_cells, S, NODES_PER_CELL)
    off_diag = leaf_y - near
    basis_rows = orthonormal(off_diag)
    leaf_basis = basis_rows.transpose(1, 0, 2).reshape(S, total) * math.sqrt(NODES_PER_CELL)
    sample_hat = project(basis_rows, leaf_y)
    probe_hat = project(basis_rows, finest_cell_random_test)
    skeleton_unpruned = scratch_buffer[:, :3, ::step_width]
    skeleton = jnp.concatenate([skeleton_unpruned[:, :2], step_width * skeleton_unpruned[:, 2:]], 1)
    for level in range(LEAF_LEVELS + CROSS):
        off_diag, joined_y, joined_w, skeleton = assemble(sample_hat, probe_hat, skeleton)
        basis_rows = orthonormal(off_diag)
        sample_hat = project(basis_rows, joined_y)
        probe_hat = project(basis_rows, joined_w)
    top_basis = jnp.repeat(basis_rows, 2 ** CROSS, axis=0) * math.sqrt(2 * S)
    return (leaf_basis, top_basis)
```

```python
import functools
import math

import jax
import jax.numpy as jnp
from jax import lax
from jax.experimental import pallas as pl
from jax.experimental.pallas import tpu as pltpu
from jax.sharding import PartitionSpec as P

NODES_PER_CELL = 512
S = 128
LEAF_LEVELS = 4
CROSS = 3
PANEL = 32
GROUP = 8
HIGHEST = lax.Precision.HIGHEST
LOG_SCALE = -0.25 / math.pi
VMEM_LIMIT = 60000 * 1024


def matmul(a, b, contract=(1, 0)):
    return lax.dot_general(
        a,
        b,
        (((contract[0],), (contract[1],)), ((), ())),
        precision=HIGHEST,
        preferred_element_type=jnp.float32,
    )


def split_bf16(value):
    high = value.astype(jnp.bfloat16)
    return high, (value - high.astype(jnp.float32)).astype(jnp.bfloat16)


def matmul_split(a, b):
    a_high, a_low = split_bf16(a)
    b_high, b_low = split_bf16(b)
    dot = functools.partial(jnp.dot, preferred_element_type=jnp.float32)
    return dot(a_high, b_high) + (dot(a_high, b_low) + dot(a_low, b_high))


def lane_cast(value, k):
    return jnp.broadcast_to(value[:, k : k + 1], value.shape)


def row_cast(value, j):
    return jnp.broadcast_to(value[j : j + 1, :], (8, value.shape[1]))


def inverse_factor(grams, work_ref):
    order = grams[0].shape[0]
    count = len(grams)
    for i, gram in enumerate(grams):
        work_ref[i] = gram
    lane = lax.broadcasted_iota(jnp.int32, (8, order), 1)
    sub = lax.broadcasted_iota(jnp.int32, (8, order), 0)
    for start in range(0, order, PANEL):
        tiles = PANEL // 8
        stop = start + PANEL
        panels = [
            [work_ref[i, start + 8 * v : start + 8 * v + 8, :] for v in range(tiles)]
            for i in range(count)
        ]
        for k in range(start, stop, GROUP):
            first = (k - start) // 8
            offset = k % 8
            in_group = (lane >= k) & (lane < k + GROUP)
            below = sub > offset + GROUP - 1
            for i in range(count):
                tile = panels[i]
                rows = [row_cast(tile[first], offset + j) for j in range(GROUP)]
                pivot = {
                    (j, l): lane_cast(rows[j], k + l)
                    for j in range(GROUP)
                    for l in range(j, GROUP)
                }
                live = [v for v in range(first, tiles) if v > first or offset + GROUP < 8]
                column = {v: [lane_cast(tile[v], k + l) for l in range(GROUP)] for v in live}
                if first in column:
                    column[first] = [jnp.where(below, c, 0.0) for c in column[first]]
                rows = [
                    jnp.where(in_group, jnp.where(lane == k + j, 1.0, 0.0), rows[j])
                    for j in range(GROUP)
                ]
                for v in range(first, tiles):
                    tile[v] = jnp.where(in_group, 0.0, tile[v])
                scaled = []
                for j in range(GROUP):
                    diagonal = pivot[j, j]
                    reciprocal = 1.0 / diagonal
                    for l in range(j + 1, GROUP):
                        factor = pivot[j, l] * reciprocal
                        rows[l] = rows[l] - factor * rows[j]
                        for q in range(l, GROUP):
                            pivot[l, q] = pivot[l, q] - factor * pivot[j, q]
                    for v in live:
                        multiplier = column[v][j] * reciprocal
                        for l in range(j + 1, GROUP):
                            column[v][l] = column[v][l] - multiplier * pivot[j, l]
                        tile[v] = tile[v] - multiplier * rows[j]
                    root = lax.rsqrt(diagonal)
                    root = root * (1.5 - 0.5 * diagonal * root * root)
                    scaled.append(rows[j] * root)
                for j in range(GROUP):
                    tile[first] = jnp.where(sub == offset + j, scaled[j], tile[first])
        for i in range(count):
            panel = jnp.concatenate(panels[i], 0)
            lanes = lax.broadcasted_iota(jnp.int32, panel.shape, 1)
            places = lax.broadcasted_iota(jnp.int32, panel.shape, 0) + start
            above = lanes > places
            work_ref[i, start:stop, :] = jnp.where(above, 0.0, panel)
            if stop < order:
                kept = jnp.where(above & (lanes < stop), 0.0, panel)
                rest = work_ref[i, stop:, :]
                rest_lanes = lax.broadcasted_iota(jnp.int32, rest.shape, 1)
                cleared = jnp.where((rest_lanes >= start) & (rest_lanes < stop), 0.0, rest)
                work_ref[i, stop:, :] = cleared - matmul(panel.T[stop:, :], kept)


def log_kernel(source_cols, target_rows):
    delta_x = source_cols[:, 0:1] - target_rows[0:1, :]
    delta_y = source_cols[:, 1:2] - target_rows[1:2, :]
    return jnp.log(delta_x * delta_x + delta_y * delta_y) * LOG_SCALE


def near_kernel(rows_ref, *refs):
    col_refs, scale_refs, probe_refs, out_ref = refs[:3], refs[3:6], refs[6:9], refs[9]
    span = out_ref.shape[1]
    target = rows_ref[...]
    weight = scale_refs[1][2:3, :]
    self_term = (1.0 - jnp.log(0.5 * weight)) * (0.5 / math.pi)
    total = probe_refs[1][...] * (self_term * weight)
    for place in range(3):
        cols = col_refs[place][...]
        delta_x = cols[:, 0:1] - target[0:1, :]
        delta_y = cols[:, 1:2] - target[1:2, :]
        squared = delta_x * delta_x + delta_y * delta_y
        if place == 1:
            own = lax.broadcasted_iota(jnp.int32, (span, span), 0) == lax.broadcasted_iota(
                jnp.int32, (span, span), 1
            )
            squared = jnp.where(own, 1.0, squared)
        weighted = probe_refs[place][...] * (scale_refs[place][2:3, :] * LOG_SCALE)
        total = total + matmul_split(weighted, jnp.log(squared))
    out_ref[...] = total


def near_field(rows, cols, probe, leaf_count):
    span = NODES_PER_CELL
    columns = probe.shape[0]

    def lanes(height, shift):
        return pl.BlockSpec((height, span), lambda t: (0, t + shift))

    return pl.pallas_call(
        near_kernel,
        grid=(leaf_count,),
        out_shape=jax.ShapeDtypeStruct((columns, leaf_count * span), jnp.float32),
        in_specs=[lanes(3, 1)]
        + [pl.BlockSpec((span, 2), lambda t, shift=shift: (t + shift, 0)) for shift in range(3)]
        + [lanes(3, shift) for shift in range(3)]
        + [lanes(columns, shift) for shift in range(3)],
        out_specs=pl.BlockSpec((columns, span), lambda t: (0, t)),
        compiler_params=pltpu.CompilerParams(vmem_limit_bytes=VMEM_LIMIT),
        name="near_field",
    )(rows, cols, cols, cols, rows, rows, rows, probe, probe, probe)


def off_diagonal(y_a, y_b, w_a, w_b, rows_a, rows_b, cols_b):
    potential = log_kernel(cols_b, rows_a)
    z_a = y_a - matmul(w_b * rows_b[2:3, :], potential)
    z_b = y_b - matmul(w_a * rows_a[2:3, :], potential, (1, 1))
    return z_a, z_b


def local_kernel(levels, leaf_count, *refs):
    near_ref, sketch_ref, probe_ref = refs[:3]
    skeleton_refs = refs[3 : 3 + 2 * levels]
    basis_ref, y_out_ref, w_out_ref, work_ref = refs[3 + 2 * levels :]
    span = NODES_PER_CELL
    blocks = []
    for t in range(leaf_count):
        at = slice(t * span, (t + 1) * span)
        y = sketch_ref[:, at]
        z = y - near_ref[:, at]
        blocks.append((z, y, probe_ref[:, at.start + span : at.stop + span]))
    products = [
        [matmul(part, z, (1, 1)) for part in (z, y, w)] for z, y, w in blocks
    ]
    inverse_factor([p[0] for p in products], work_ref)
    for t, (z, _, _) in enumerate(blocks):
        basis_ref[:, t * span : (t + 1) * span] = matmul(work_ref[t], z) * math.sqrt(span)
    hats = [
        (matmul(p[1], work_ref[t], (1, 1)), matmul(p[2], work_ref[t], (1, 1)))
        for t, p in enumerate(products)
    ]
    for level in range(levels):
        rows, cols = skeleton_refs[2 * level], skeleton_refs[2 * level + 1]
        products = []
        for a in range(0, len(hats), 2):
            at_a, at_b = slice(a * S, (a + 1) * S), slice((a + 1) * S, (a + 2) * S)
            (y_a, w_a), (y_b, w_b) = hats[a], hats[a + 1]
            z_a, z_b = off_diagonal(
                y_a, y_b, w_a, w_b, rows[:, at_a], rows[:, at_b], cols[at_b, :]
            )
            products.append(pair_products(z_a, z_b, y_a, y_b, w_a, w_b))
        inverse_factor([p[0] for p in products], work_ref)
        hats = [
            (matmul(p[1], work_ref[t], (1, 1)), matmul(p[2], work_ref[t], (1, 1)))
            for t, p in enumerate(products)
        ]
    y_out_ref[...] = hats[0][0]
    w_out_ref[...] = hats[0][1]


def pair_products(z_a, z_b, y_a, y_b, w_a, w_b):
    return [
        matmul(a, z_a, (1, 1)) + matmul(b, z_b, (1, 1))
        for a, b in ((z_a, z_b), (y_a, y_b), (w_a, w_b))
    ]


def pair_kernel(last, mine_ref, other_ref, rows_m_ref, rows_o_ref, cols_o_ref, out_ref, work_ref):
    y_m, w_m, y_o, w_o = mine_ref[0], mine_ref[1], other_ref[0], other_ref[1]
    z_m, z_o = off_diagonal(
        y_m, y_o, w_m, w_o, rows_m_ref[...], rows_o_ref[...], cols_o_ref[...]
    )
    if last:
        gram = matmul(z_m, z_m, (1, 1)) + matmul(z_o, z_o, (1, 1))
        inverse_factor([gram], work_ref)
        out_ref[0] = matmul(work_ref[0], z_m)
        out_ref[1] = matmul(work_ref[0], z_o)
    else:
        gram, y_z, w_z = pair_products(z_m, z_o, y_m, y_o, w_m, w_o)
        inverse_factor([gram], work_ref)
        out_ref[0] = matmul(y_z, work_ref[0], (1, 1))
        out_ref[1] = matmul(w_z, work_ref[0], (1, 1))


def merge_pair(mine, other, rows_m, rows_o, last):
    return pl.pallas_call(
        functools.partial(pair_kernel, last),
        out_shape=jax.ShapeDtypeStruct((2, S, S), jnp.float32),
        scratch_shapes=[pltpu.VMEM((1, S, S), jnp.float32)],
        name="merge_last" if last else "merge_pair",
    )(mine, other, rows_m, rows_o, rows_o[:2].T)


def from_partner(block, axis, stride):
    count = lax.axis_size(axis)
    route = []
    for low in range(count):
        high = low | 1 << stride
        if high != low and high < count:
            route += [(low, high), (high, low)]
    return lax.ppermute(block, axis, route)


def with_halo(block, axis, width):
    count = lax.axis_size(axis)
    forward = [(i, (i + 1) % count) for i in range(count)]
    backward = [(target, source) for source, target in forward]
    low = lax.ppermute(block[:, block.shape[1] - width :], axis, forward)
    high = lax.ppermute(block[:, :width], axis, backward)
    return jnp.concatenate([low, block, high], axis=1)


def body(curve_coordinates, weighted_density, random_test_matrix, sketch_matrix):
    span = NODES_PER_CELL
    columns, width = random_test_matrix.shape
    ranks = lax.axis_size("rep")
    rank = lax.axis_index("rep")
    leaf_count = width // span // ranks
    levels = leaf_count.bit_length() - 1
    chunk = leaf_count * span
    step = span // S

    sketch = lax.all_to_all(sketch_matrix, "rep", split_axis=1, concat_axis=0, tiled=True)
    points = jnp.concatenate([curve_coordinates, weighted_density[None, :]], 0)
    padded = with_halo(jnp.concatenate([points, random_test_matrix], 0), "leaf", span)
    windows = jnp.concatenate(
        [padded[3:, r * chunk : (r + 1) * chunk + 2 * span] for r in range(ranks)], 1
    )
    probe = lax.all_to_all(windows, "rep", split_axis=1, concat_axis=0, tiled=True)
    rows = lax.dynamic_slice_in_dim(padded[:3], rank * chunk, chunk + 2 * span, 1)
    near = near_field(rows, rows[:2].T, probe, leaf_count)

    def skeleton_of(source, level):
        stride = step << level
        taken = source[:, ::stride]
        return jnp.concatenate([taken[:2], stride * taken[2:]], 0)

    inner = rows[:, span : span + chunk]
    local = []
    for level in range(levels):
        taken = skeleton_of(inner, level)
        local += [taken, taken[:2].T]
    basis, y_hat, w_hat = pl.pallas_call(
        functools.partial(local_kernel, levels, leaf_count),
        out_shape=(
            jax.ShapeDtypeStruct((S, chunk), jnp.float32),
            jax.ShapeDtypeStruct((S, S), jnp.float32),
            jax.ShapeDtypeStruct((S, S), jnp.float32),
        ),
        scratch_shapes=[pltpu.VMEM((leaf_count, S, S), jnp.float32)],
        compiler_params=pltpu.CompilerParams(vmem_limit_bytes=VMEM_LIMIT),
        name="local_levels",
    )(near, sketch, probe, *local)
    leaf_basis = lax.all_to_all(basis, "rep", split_axis=0, concat_axis=1, tiled=True)

    hats = jnp.stack([y_hat, w_hat])
    for level in range(LEAF_LEVELS - levels):
        taken = skeleton_of(points, levels + level)
        node = rank >> level
        mine = lax.dynamic_slice_in_dim(taken, node * S, S, 1)
        theirs = lax.dynamic_slice_in_dim(taken, (node ^ 1) * S, S, 1)
        hats = merge_pair(hats, from_partner(hats, "rep", level), mine, theirs, False)
    position = lax.axis_index("leaf")
    mine = skeleton_of(points, LEAF_LEVELS)
    for level in range(CROSS):
        theirs = from_partner(mine, "leaf", level)
        second = (position >> level) % 2 == 1
        hats = merge_pair(
            hats, from_partner(hats, "leaf", level), mine, theirs, level == CROSS - 1
        )
        joined = jnp.where(
            second,
            jnp.concatenate([theirs, mine], 1),
            jnp.concatenate([mine, theirs], 1),
        )[:, ::2]
        mine = jnp.concatenate([joined[:2], 2.0 * joined[2:]], 0)
    top = lax.dynamic_slice_in_dim(hats, rank * columns, columns, 1) * math.sqrt(2 * S)
    top = jnp.where(
        second, jnp.concatenate([top[1], top[0]], 1), jnp.concatenate([top[0], top[1]], 1)
    )
    return (leaf_basis, top[None])


def solution(mesh):
    return jax.shard_map(
        body,
        mesh=mesh,
        in_specs=(P(None, "leaf"), P("leaf"), P("rep", "leaf"), P("rep", "leaf")),
        out_specs=(P("rep", "leaf"), P("leaf", "rep", None)),
        check_vma=False,
    )
```

```python
import functools
import math

import jax
import jax.numpy as jnp
from jax import lax
from jax.experimental import pallas as pl
from jax.experimental.pallas import tpu as pltpu
from jax.sharding import PartitionSpec as P

NODES_PER_CELL = 512
S = 128
LEAF_LEVELS = 4
CROSS = 3
PANEL = 32
GROUP = 8
HIGHEST = lax.Precision.HIGHEST
LOG_SCALE = -0.25 / math.pi
VMEM_LIMIT = 60000 * 1024


def matmul(a, b, contract=(1, 0)):
    return lax.dot_general(
        a,
        b,
        (((contract[0],), (contract[1],)), ((), ())),
        precision=HIGHEST,
        preferred_element_type=jnp.float32,
    )


def split_bf16(value):
    high = value.astype(jnp.bfloat16)
    return high, (value - high.astype(jnp.float32)).astype(jnp.bfloat16)


def matmul_split(a, b):
    a_high, a_low = split_bf16(a)
    b_high, b_low = split_bf16(b)
    dot = functools.partial(jnp.dot, preferred_element_type=jnp.float32)
    return dot(a_high, b_high) + (dot(a_high, b_low) + dot(a_low, b_high))


def lane_cast(value, k):
    return jnp.broadcast_to(value[:, k : k + 1], value.shape)


def row_cast(value, j):
    return jnp.broadcast_to(value[j : j + 1, :], (8, value.shape[1]))


def inverse_factor(grams, work_ref):
    order = grams[0].shape[0]
    count = len(grams)
    for i, gram in enumerate(grams):
        work_ref[i] = gram
    lane = lax.broadcasted_iota(jnp.int32, (8, order), 1)
    sub = lax.broadcasted_iota(jnp.int32, (8, order), 0)
    for start in range(0, order, PANEL):
        tiles = PANEL // 8
        stop = start + PANEL
        panels = [
            [work_ref[i, start + 8 * v : start + 8 * v + 8, :] for v in range(tiles)]
            for i in range(count)
        ]
        for k in range(start, stop, GROUP):
            first = (k - start) // 8
            offset = k % 8
            in_group = (lane >= k) & (lane < k + GROUP)
            below = sub > offset + GROUP - 1
            for i in range(count):
                tile = panels[i]
                rows = [row_cast(tile[first], offset + j) for j in range(GROUP)]
                pivot = {
                    (j, l): lane_cast(rows[j], k + l)
                    for j in range(GROUP)
                    for l in range(j, GROUP)
                }
                live = [v for v in range(first, tiles) if v > first or offset + GROUP < 8]
                column = {v: [lane_cast(tile[v], k + l) for l in range(GROUP)] for v in live}
                if first in column:
                    column[first] = [jnp.where(below, c, 0.0) for c in column[first]]
                rows = [
                    jnp.where(in_group, jnp.where(lane == k + j, 1.0, 0.0), rows[j])
                    for j in range(GROUP)
                ]
                for v in range(first, tiles):
                    tile[v] = jnp.where(in_group, 0.0, tile[v])
                scaled = []
                for j in range(GROUP):
                    diagonal = pivot[j, j]
                    reciprocal = 1.0 / diagonal
                    for l in range(j + 1, GROUP):
                        factor = pivot[j, l] * reciprocal
                        rows[l] = rows[l] - factor * rows[j]
                        for q in range(l, GROUP):
                            pivot[l, q] = pivot[l, q] - factor * pivot[j, q]
                    for v in live:
                        multiplier = column[v][j] * reciprocal
                        for l in range(j + 1, GROUP):
                            column[v][l] = column[v][l] - multiplier * pivot[j, l]
                        tile[v] = tile[v] - multiplier * rows[j]
                    root = lax.rsqrt(diagonal)
                    root = root * (1.5 - 0.5 * diagonal * root * root)
                    scaled.append(rows[j] * root)
                for j in range(GROUP):
                    tile[first] = jnp.where(sub == offset + j, scaled[j], tile[first])
        for i in range(count):
            panel = jnp.concatenate(panels[i], 0)
            lanes = lax.broadcasted_iota(jnp.int32, panel.shape, 1)
            places = lax.broadcasted_iota(jnp.int32, panel.shape, 0) + start
            above = lanes > places
            work_ref[i, start:stop, :] = jnp.where(above, 0.0, panel)
            if stop < order:
                kept = jnp.where(above & (lanes < stop), 0.0, panel)
                rest = work_ref[i, stop:, :]
                rest_lanes = lax.broadcasted_iota(jnp.int32, rest.shape, 1)
                cleared = jnp.where((rest_lanes >= start) & (rest_lanes < stop), 0.0, rest)
                work_ref[i, stop:, :] = cleared - matmul(panel.T[stop:, :], kept)


def log_kernel(source_cols, target_rows):
    delta_x = source_cols[:, 0:1] - target_rows[0:1, :]
    delta_y = source_cols[:, 1:2] - target_rows[1:2, :]
    return jnp.log(delta_x * delta_x + delta_y * delta_y) * LOG_SCALE


def near_kernel(rows_ref, *refs):
    col_refs, scale_refs, probe_refs, out_ref = refs[:3], refs[3:6], refs[6:9], refs[9]
    span = out_ref.shape[1]
    target = rows_ref[...]
    weight = scale_refs[1][2:3, :]
    self_term = (1.0 - jnp.log(0.5 * weight)) * (0.5 / math.pi)
    total = probe_refs[1][...] * (self_term * weight)
    for place in range(3):
        cols = col_refs[place][...]
        delta_x = cols[:, 0:1] - target[0:1, :]
        delta_y = cols[:, 1:2] - target[1:2, :]
        squared = delta_x * delta_x + delta_y * delta_y
        if place == 1:
            own = lax.broadcasted_iota(jnp.int32, (span, span), 0) == lax.broadcasted_iota(
                jnp.int32, (span, span), 1
            )
            squared = jnp.where(own, 1.0, squared)
        weighted = probe_refs[place][...] * (scale_refs[place][2:3, :] * LOG_SCALE)
        total = total + matmul_split(weighted, jnp.log(squared))
    out_ref[...] = total


def near_field(rows, cols, probe, leaf_count):
    span = NODES_PER_CELL
    columns = probe.shape[0]

    def lanes(height, shift):
        return pl.BlockSpec((height, span), lambda t: (0, t + shift))

    return pl.pallas_call(
        near_kernel,
        grid=(leaf_count,),
        out_shape=jax.ShapeDtypeStruct((columns, leaf_count * span), jnp.float32),
        in_specs=[lanes(3, 1)]
        + [pl.BlockSpec((span, 2), lambda t, shift=shift: (t + shift, 0)) for shift in range(3)]
        + [lanes(3, shift) for shift in range(3)]
        + [lanes(columns, shift) for shift in range(3)],
        out_specs=pl.BlockSpec((columns, span), lambda t: (0, t)),
        compiler_params=pltpu.CompilerParams(vmem_limit_bytes=VMEM_LIMIT),
        name="near_field",
    )(rows, cols, cols, cols, rows, rows, rows, probe, probe, probe)


def off_diagonal(y_a, y_b, w_a, w_b, rows_a, rows_b, cols_b):
    potential = log_kernel(cols_b, rows_a)
    z_a = y_a - matmul(w_b * rows_b[2:3, :], potential)
    z_b = y_b - matmul(w_a * rows_a[2:3, :], potential, (1, 1))
    return z_a, z_b


def local_kernel(levels, leaf_count, *refs):
    near_ref, sketch_ref, probe_ref = refs[:3]
    skeleton_refs = refs[3 : 3 + 2 * levels]
    basis_ref, hats_ref, work_ref = refs[3 + 2 * levels :]
    span = NODES_PER_CELL
    blocks = []
    for t in range(leaf_count):
        at = slice(t * span, (t + 1) * span)
        y = sketch_ref[:, at]
        z = y - near_ref[:, at]
        blocks.append((z, y, probe_ref[:, at.start + span : at.stop + span]))
    products = [
        [matmul(part, z, (1, 1)) for part in (z, y, w)] for z, y, w in blocks
    ]
    inverse_factor([p[0] for p in products], work_ref)
    for t, (z, _, _) in enumerate(blocks):
        basis_ref[:, t * span : (t + 1) * span] = matmul(work_ref[t], z) * math.sqrt(span)
    hats = [
        (matmul(p[1], work_ref[t], (1, 1)), matmul(p[2], work_ref[t], (1, 1)))
        for t, p in enumerate(products)
    ]
    for level in range(levels):
        rows, cols = skeleton_refs[2 * level], skeleton_refs[2 * level + 1]
        products = []
        for a in range(0, len(hats), 2):
            at_a, at_b = slice(a * S, (a + 1) * S), slice((a + 1) * S, (a + 2) * S)
            (y_a, w_a), (y_b, w_b) = hats[a], hats[a + 1]
            z_a, z_b = off_diagonal(
                y_a, y_b, w_a, w_b, rows[:, at_a], rows[:, at_b], cols[at_b, :]
            )
            products.append(pair_products(z_a, z_b, y_a, y_b, w_a, w_b))
        inverse_factor([p[0] for p in products], work_ref)
        hats = [
            (matmul(p[1], work_ref[t], (1, 1)), matmul(p[2], work_ref[t], (1, 1)))
            for t, p in enumerate(products)
        ]
    hats_ref[0] = hats[0][0]
    hats_ref[1] = hats[0][1]


def pair_products(z_a, z_b, y_a, y_b, w_a, w_b):
    return [
        matmul(a, z_a, (1, 1)) + matmul(b, z_b, (1, 1))
        for a, b in ((z_a, z_b), (y_a, y_b), (w_a, w_b))
    ]


def peer_of(stride):
    ranks = lax.axis_size("rep")
    place = lax.axis_index("leaf") * ranks + lax.axis_index("rep")
    peer = place + stride * (1 - 2 * ((place // stride) % 2))
    return (peer // ranks, peer % ranks)


def merge_kernel(
    levels,
    hats_ref,
    rows_m_ref,
    rows_o_ref,
    cols_o_ref,
    out_ref,
    mine_ref,
    other_ref,
    work_ref,
    load_sem,
    send_sem,
    recv_sem,
):
    barrier = pltpu.get_barrier_semaphore()
    for level in range(levels):
        pl.semaphore_signal(
            barrier, inc=1, device_id=peer_of(1 << level), device_id_type=pl.DeviceIdType.MESH
        )
    load = pltpu.make_async_copy(hats_ref, mine_ref.at[0], load_sem)
    load.start()
    load.wait()
    pl.semaphore_wait(barrier, levels)

    def exchange(level, stride):
        copy = pltpu.make_async_remote_copy(
            src_ref=mine_ref.at[level],
            dst_ref=other_ref.at[level],
            send_sem=send_sem.at[level],
            recv_sem=recv_sem.at[level],
            device_id=peer_of(stride),
            device_id_type=pl.DeviceIdType.MESH,
        )
        copy.start()
        rows_m, rows_o = rows_m_ref[level], rows_o_ref[level]
        potential = log_kernel(cols_o_ref[level], rows_m)
        copy.wait()
        y_m, w_m = mine_ref[level, 0], mine_ref[level, 1]
        y_o, w_o = other_ref[level, 0], other_ref[level, 1]
        z_m = y_m - matmul(w_o * rows_o[2:3, :], potential)
        z_o = y_o - matmul(w_m * rows_m[2:3, :], potential, (1, 1))
        return z_m, z_o, y_m, y_o, w_m, w_o

    def step(level, stride):
        gram, y_z, w_z = pair_products(*exchange(level, stride))
        inverse_factor([gram], work_ref)
        mine_ref[level + 1, 0] = matmul(y_z, work_ref[0], (1, 1))
        mine_ref[level + 1, 1] = matmul(w_z, work_ref[0], (1, 1))
        return stride * 2

    stride = lax.fori_loop(0, levels - 1, step, 1)
    z_m, z_o = exchange(levels - 1, stride)[:2]
    gram = matmul(z_m, z_m, (1, 1)) + matmul(z_o, z_o, (1, 1))
    inverse_factor([gram], work_ref)
    columns = out_ref.shape[0]
    start = pl.multiple_of(lax.axis_index("rep") * columns, 8)
    factor = work_ref[0, pl.ds(start, columns), :] * math.sqrt(2 * S)
    second = (lax.axis_index("leaf") // (1 << (CROSS - 1))) % 2 == 1
    out_ref[:, :S] = matmul(factor, jnp.where(second, z_o, z_m))
    out_ref[:, S:] = matmul(factor, jnp.where(second, z_m, z_o))


def merge_levels(hats, rows_m, rows_o, columns):
    levels = len(rows_m)
    vmem = pl.BlockSpec(memory_space=pltpu.VMEM)
    return pl.pallas_call(
        functools.partial(merge_kernel, levels),
        out_shape=jax.ShapeDtypeStruct((columns, 2 * S), jnp.float32),
        in_specs=[pl.BlockSpec(memory_space=pl.ANY), vmem, vmem, vmem],
        out_specs=vmem,
        scratch_shapes=[
            pltpu.VMEM((levels, 2, S, S), jnp.float32),
            pltpu.VMEM((levels, 2, S, S), jnp.float32),
            pltpu.VMEM((1, S, S), jnp.float32),
            pltpu.SemaphoreType.DMA,
            pltpu.SemaphoreType.DMA((levels,)),
            pltpu.SemaphoreType.DMA((levels,)),
        ],
        compiler_params=pltpu.CompilerParams(collective_id=0, has_side_effects=True),
        name="merge_levels",
    )(
        hats,
        jnp.stack(rows_m),
        jnp.stack(rows_o),
        jnp.stack([taken[:2].T for taken in rows_o]),
    )


def from_partner(block, axis, stride):
    count = lax.axis_size(axis)
    route = []
    for low in range(count):
        high = low | 1 << stride
        if high != low and high < count:
            route += [(low, high), (high, low)]
    return lax.ppermute(block, axis, route)


def with_halo(block, axis, width):
    count = lax.axis_size(axis)
    forward = [(i, (i + 1) % count) for i in range(count)]
    backward = [(target, source) for source, target in forward]
    low = lax.ppermute(block[:, block.shape[1] - width :], axis, forward)
    high = lax.ppermute(block[:, :width], axis, backward)
    return jnp.concatenate([low, block, high], axis=1)


def body(curve_coordinates, weighted_density, random_test_matrix, sketch_matrix):
    span = NODES_PER_CELL
    columns, width = random_test_matrix.shape
    ranks = lax.axis_size("rep")
    rank = lax.axis_index("rep")
    leaf_count = width // span // ranks
    levels = leaf_count.bit_length() - 1
    chunk = leaf_count * span
    step = span // S

    sketch = lax.all_to_all(sketch_matrix, "rep", split_axis=1, concat_axis=0, tiled=True)
    points = jnp.concatenate([curve_coordinates, weighted_density[None, :]], 0)
    padded = with_halo(jnp.concatenate([points, random_test_matrix], 0), "leaf", span)
    windows = jnp.concatenate(
        [padded[3:, r * chunk : (r + 1) * chunk + 2 * span] for r in range(ranks)], 1
    )
    probe = lax.all_to_all(windows, "rep", split_axis=1, concat_axis=0, tiled=True)
    rows = lax.dynamic_slice_in_dim(padded[:3], rank * chunk, chunk + 2 * span, 1)
    near = near_field(rows, rows[:2].T, probe, leaf_count)

    def skeleton_of(source, level):
        stride = step << level
        taken = source[:, ::stride]
        return jnp.concatenate([taken[:2], stride * taken[2:]], 0)

    inner = rows[:, span : span + chunk]
    local = []
    for level in range(levels):
        taken = skeleton_of(inner, level)
        local += [taken, taken[:2].T]
    basis, hats = pl.pallas_call(
        functools.partial(local_kernel, levels, leaf_count),
        out_shape=(
            jax.ShapeDtypeStruct((S, chunk), jnp.float32),
            jax.ShapeDtypeStruct((2, S, S), jnp.float32),
        ),
        scratch_shapes=[pltpu.VMEM((leaf_count, S, S), jnp.float32)],
        compiler_params=pltpu.CompilerParams(vmem_limit_bytes=VMEM_LIMIT),
        name="local_levels",
    )(near, sketch, probe, *local)
    leaf_basis = lax.all_to_all(basis, "rep", split_axis=0, concat_axis=1, tiled=True)

    rows_m, rows_o = [], []
    for level in range(LEAF_LEVELS - levels):
        taken = skeleton_of(points, levels + level)
        node = rank >> level
        rows_m.append(lax.dynamic_slice_in_dim(taken, node * S, S, 1))
        rows_o.append(lax.dynamic_slice_in_dim(taken, (node ^ 1) * S, S, 1))
    position = lax.axis_index("leaf")
    mine = skeleton_of(points, LEAF_LEVELS)
    for level in range(CROSS):
        theirs = from_partner(mine, "leaf", level)
        rows_m.append(mine)
        rows_o.append(theirs)
        joined = jnp.where(
            (position >> level) % 2 == 1,
            jnp.concatenate([theirs, mine], 1),
            jnp.concatenate([mine, theirs], 1),
        )[:, ::2]
        mine = jnp.concatenate([joined[:2], 2.0 * joined[2:]], 0)
    top = merge_levels(hats, rows_m, rows_o, columns)
    return (leaf_basis, top[None])


def solution(mesh):
    return jax.shard_map(
        body,
        mesh=mesh,
        in_specs=(P(None, "leaf"), P("leaf"), P("rep", "leaf"), P("rep", "leaf")),
        out_specs=(P("rep", "leaf"), P("leaf", "rep", None)),
        check_vma=False,
    )
```
